128 devices in a mesh: obs: 8 (over z_lo, y), tm: 16 (over x, z_hi, core).
Axes of the slice: x: 4, y: 4, z: 4 (z_hi: 2, z_lo: 2; z = z_hi * 2 + z_lo), core: 2. Of those that a mesh axis runs over, the one named last changes fastest.
Arguments:
- footprints: bfloat16 [4096, 16, 2048], P('obs', 'tm'), may hold values from -0.125 to 0.125
- spatial_cov: bfloat16 [2048, 2048], replicated, may hold values from -2 to 11, as said below
- time_cov: float32 [16, 16], replicated, may hold values from -1 to 3, as said below
- flux_draws: bfloat16 [256, 16, 2048], P('obs', 'tm'), may hold values from -6 to 6
- perturbed: float32 [4096, 256], P('obs'), may hold values from -96 to 96
- obs_error: float32 [4096], P('obs'), may hold values from 16 to 64
Outputs:
- weights: float32 [4096, 256], P(('obs', 'tm'))
- update: float32 [256, 16, 2048], P('obs', 'tm')
The draws below stay inside these ranges and needn't reach their ends.
Inputs may be any that keep to these rules, and one draw needn't show every extreme that they name: `spatial_cov`: symmetric. `time_cov`: symmetric.
All inputs are finite; a program needn't handle non-finite values.
Results may differ from the reference program's by a relative error of at most 0.0059.
Values may be sent and summed in bfloat16 or wider, within the bound.
A program may use at most 128 MiB of HBM per device.

```python
import math
import jax
import jax.numpy as jnp
from jax import lax

CELLS = 2048
DRAWS = 256
SWEEPS = 2
PERIODS = 16
OBS = 4096


def draw_spatial_cov(key, part):
    first = jax.random.fold_in(key, 11)
    second = jax.random.fold_in(key, 12)
    normal = jnp.clip(jax.random.normal(first, (CELLS, CELLS), jnp.float32), -4.0, 4.0)
    noise = 0.5 * (normal + normal.T) / math.sqrt(2.0 * CELLS)
    raised = jnp.diag(1.5 + jax.random.uniform(second, (CELLS,), jnp.float32))
    matrix = raised + noise
    return matrix.astype(jnp.bfloat16)


def draw_time_cov(key, part):
    first = jax.random.fold_in(key, 21)
    second = jax.random.fold_in(key, 22)
    values = jax.random.uniform(first, (PERIODS, PERIODS), jnp.float32, -1.732, 1.732)
    noise = 0.4 * (values + values.T) / math.sqrt(2.0 * PERIODS)
    raised = jnp.diag(1.0 + jax.random.uniform(second, (PERIODS,), jnp.float32))
    return raised + noise


def level_of(rng, extent, pieces, smallest, top_value):
    level, own = 1.0, jax.random.fold_in(rng, 6)
    for axis_at, shards_of in pieces:
        heights = jnp.exp(jax.random.uniform(jax.random.fold_in(own, axis_at), (shards_of,), jnp.float32, smallest / len(pieces), top_value / len(pieces)))
        level = level * jnp.repeat(heights, extent[axis_at] // shards_of).reshape([-1 if axis == axis_at else 1 for axis in range(len(extent))])
    return level


def gaussian(key, dims, width, reach, shards=(), kind=jnp.bfloat16):
    drawn = width * jax.random.normal(key, dims, jnp.float32)
    if shards:
        drawn = drawn * level_of(key, dims, shards, -0.22, 0.18)
    return jnp.clip(drawn, -reach, reach).astype(kind)


def setup_inputs(seed: int = 0) -> dict:
    key_of = jax.random.split(jax.random.key(seed), 7)
    return {
        "footprints": gaussian(key_of[0], (OBS, PERIODS, CELLS), CELLS ** -0.5, 0.125, ((0, 8), (1, 16))),
        "spatial_cov": draw_spatial_cov(jax.random.fold_in(key_of[6], 71), 0),
        "time_cov": draw_time_cov(jax.random.fold_in(key_of[6], 71), 0),
        "flux_draws": gaussian(key_of[3], (DRAWS, PERIODS, CELLS), 1.0, 6.0, ((0, 8), (1, 16))),
        "perturbed": gaussian(key_of[4], (OBS, DRAWS), PERIODS, 96.0, ((0, 8),), jnp.float32),
        "obs_error": jnp.clip(jnp.exp(math.log(64.0) - 1.3862944 * jax.random.uniform(key_of[5], (OBS,), jnp.float32) ** level_of(key_of[5], (OBS,), ((0, 8),), -0.2, 0.2)), 16.0, 64.0),
    }


def contract_last(left, right):
    return lax.dot_general(left, right, (((1,), (1,)), ((), ())), preferred_element_type=jnp.float32)


def reference(footprints, spatial_cov, time_cov, flux_draws, perturbed, obs_error):
    flat = footprints.reshape(OBS * PERIODS, CELLS)
    spread = jnp.dot(flat, spatial_cov, preferred_element_type=jnp.float32).astype(jnp.bfloat16)
    spread = spread.reshape(OBS, PERIODS, CELLS)
    mixed = jnp.einsum("ntm,ts->nsm", spread.astype(jnp.float32), time_cov, precision=lax.Precision.HIGHEST).astype(jnp.bfloat16)
    foot_wide = footprints.reshape(OBS, PERIODS * CELLS)
    mixed_wide = mixed.reshape(OBS, PERIODS * CELLS)
    covariance = contract_last(mixed_wide, foot_wide)
    predicted = contract_last(foot_wide, flux_draws.reshape(DRAWS, PERIODS * CELLS))
    residual = perturbed - predicted
    divisor = jnp.diagonal(covariance) + obs_error
    weights = residual / divisor[:, None]
    for sweep_index in range(SWEEPS):
        product = jnp.dot(covariance, weights, precision=lax.Precision.HIGHEST)
        weights = weights + (residual - product - obs_error[:, None] * weights) / divisor[:, None]
    update = lax.dot_general(weights.astype(jnp.bfloat16), mixed_wide, (((0,), (0,)), ((), ())), preferred_element_type=jnp.float32)
    return weights, update.reshape(DRAWS, PERIODS, CELLS)
```

```python
import functools

import jax
import jax.numpy as jnp
from jax import lax
from jax.experimental import pallas as pl
from jax.experimental.pallas import tpu as pltpu
from jax.sharding import PartitionSpec as P

SWEEPS = 2
MESH = pl.DeviceIdType.MESH
BF16 = jnp.bfloat16
F32 = jnp.float32
TILE = 256
BATCHES = 4


def dot_nt(left, right):
    return lax.dot_general(left, right, (((1,), (1,)), ((), ())), preferred_element_type=F32)


def dot_nn(left, right):
    return jnp.dot(left, right, preferred_element_type=F32)


def rows_at(start, size):
    return pl.ds(pl.multiple_of(start, size), size)


def kernel(
    n_obs, n_tm,
    f_ref, s_ref, t_ref, d_ref, p_ref, e_ref,
    w_ref, u_ref,
    f_v, s_v, frow, spread, mrow, mixed, dall, psend, prow,
    wall, wt, gp, grs, gall, ysend, yrow, k_hi, k_lo, pert, dacc,
    local_sem, send_sem, recv_sem, frecv_sem,
):
    o = lax.axis_index("obs")
    t = lax.axis_index("tm")
    rows, cells = f_ref.shape
    share = rows // n_tm
    draws = d_ref.shape[0]
    per_batch = n_tm // BATCHES

    def tm_peer(r):
        return lax.rem(t + r, n_tm)

    def tm_source(r):
        return lax.rem(t - r + n_tm, n_tm)

    def obs_peer(q):
        return lax.rem(o + q, n_obs)

    def send(src, dst, phase, axis, peer, recv=None):
        pltpu.make_async_remote_copy(
            src_ref=src, dst_ref=dst, send_sem=send_sem.at[phase],
            recv_sem=recv_sem.at[phase] if recv is None else recv,
            device_id={axis: peer}, device_id_type=MESH,
        ).start()

    def await_bytes(region, sem):
        pltpu.make_async_copy(region, region, sem).wait()

    load_s = pltpu.make_async_copy(s_ref, s_v, local_sem.at[0])
    load_f = pltpu.make_async_copy(f_ref, f_v, local_sem.at[1])
    load_p = pltpu.make_async_copy(p_ref.at[rows_at(t * share, share)], pert, local_sem.at[2])
    own_f = pltpu.make_async_copy(f_ref.at[rows_at(t * share, share)], frow.at[pl.ds(0, share)], local_sem.at[3])
    own_d = pltpu.make_async_copy(d_ref, dall.at[rows_at(o * draws, draws)], local_sem.at[4])

    barrier = pltpu.get_barrier_semaphore()

    @pl.loop(1, n_tm)
    def _(r):
        pl.semaphore_signal(barrier, inc=1, device_id={"tm": tm_peer(r)}, device_id_type=MESH)

    @pl.loop(1, n_obs)
    def _(q):
        pl.semaphore_signal(barrier, inc=1, device_id={"obs": obs_peer(q)}, device_id_type=MESH)

    load_f.start()
    own_f.start()
    own_d.start()
    load_p.start()
    load_s.start()
    pl.semaphore_wait(barrier, n_tm - 1 + n_obs - 1)

    @pl.loop(1, n_obs)
    def _(q):
        send(d_ref, dall.at[rows_at(o * draws, draws)], 0, "obs", obs_peer(q))

    @pl.loop(1, n_tm)
    def _(r):
        peer = tm_peer(r)
        send(
            f_ref.at[rows_at(peer * share, share)], frow.at[rows_at(r * share, share)],
            1, "tm", peer, frecv_sem.at[r // per_batch],
        )

    ids = lax.broadcasted_iota(jnp.int32, (rows, n_tm), 0) // share
    pick = (lax.rem(t - ids + n_tm, n_tm) == lax.broadcasted_iota(jnp.int32, (rows, n_tm), 1)).astype(F32)
    ids_t = lax.broadcasted_iota(jnp.int32, (n_tm, rows), 1) // share
    pick_t = (lax.rem(t - ids_t + n_tm, n_tm) == lax.broadcasted_iota(jnp.int32, (n_tm, rows), 0)).astype(F32)
    picked = jnp.dot(t_ref[...], pick_t, precision=lax.Precision.HIGHEST, preferred_element_type=F32)
    full = jnp.dot(pick, picked, precision=lax.Precision.HIGHEST, preferred_element_type=F32)
    row_in = lax.rem(lax.broadcasted_iota(jnp.int32, (rows, rows), 0), share)
    col_in = lax.rem(lax.broadcasted_iota(jnp.int32, (rows, rows), 1), share)
    full = jnp.where(row_in == col_in, full, 0.0)
    high = full.astype(BF16)
    k_hi[...] = high
    k_lo[...] = (full - high.astype(F32)).astype(BF16)

    load_f.wait()
    own_d.wait()
    await_bytes(dall.at[pl.ds(0, (n_obs - 1) * draws)], recv_sem.at[0])
    psend[...] = dot_nt(f_v[...], dall[...])

    @pl.loop(1, n_tm)
    def _(r):
        peer = tm_peer(r)
        send(psend.at[rows_at(peer * share, share)], prow.at[rows_at(r * share, share)], 2, "tm", peer)

    own_f.wait()
    load_s.wait()
    size = per_batch * share
    for batch in range(BATCHES):
        first = share if batch == 0 else 0
        await_bytes(frow.at[pl.ds(batch * size + first, size - first)], frecv_sem.at[batch])

        @pl.loop(0, cells // TILE)
        def _(c):
            cols = pl.ds(pl.multiple_of(c * TILE, TILE), TILE)
            here = pl.ds(batch * size, size)
            spread[here, cols] = dot_nn(frow[here, :], s_v[:, cols]).astype(BF16)

    dacc[...] = jnp.zeros_like(dacc)

    @pl.loop(0, cells // TILE)
    def _(c):
        cols = pl.ds(pl.multiple_of(c * TILE, TILE), TILE)
        block = spread[:, cols]
        out = (dot_nn(k_hi[...], block) + dot_nn(k_lo[...], block)).astype(BF16)
        mrow[:, cols] = out
        product = out.astype(F32) * frow[:, cols].astype(F32)
        dacc[...] += product.reshape(n_tm, share, TILE).sum(axis=0)

    load_p.wait()
    await_bytes(prow.at[pl.ds(share, rows - share)], recv_sem.at[2])
    predicted = psend[rows_at(t * share, share), :]
    predicted += prow[pl.ds(share, rows - share), :].reshape(n_tm - 1, share, -1).sum(axis=0)
    residual = pert[...] - predicted
    at_row = lax.broadcasted_iota(jnp.int32, (share, rows), 0) + t * share
    at_col = lax.broadcasted_iota(jnp.int32, (share, rows), 1)
    error = jnp.where(at_row == at_col, jnp.broadcast_to(e_ref[...], (share, rows)), 0.0).sum(axis=1, keepdims=True)
    divisor = dacc[...].sum(axis=1, keepdims=True) + error

    def share_weights(step, weights):
        wall[step, rows_at(t * share, share), :] = weights.astype(BF16)

        @pl.loop(1, n_tm)
        def _(r):
            here = wall.at[step, rows_at(t * share, share)]
            send(here, here, 4 + step, "tm", tm_peer(r))

    def weighted(step, matrix):
        await_bytes(wall.at[step, pl.ds(share, rows - share)], recv_sem.at[4 + step])
        wt[...] = wall[step].T

        @pl.loop(0, cells // TILE)
        def _(c):
            cols = pl.ds(pl.multiple_of(c * TILE, TILE), TILE)
            gp[step, :, cols] = dot_nn(wt[...], matrix[:, cols]).astype(BF16)

        @pl.loop(1, n_obs)
        def _(q):
            peer = obs_peer(q)
            send(
                gp.at[step, rows_at(peer * draws, draws)], grs.at[step, rows_at(q * draws, draws)],
                7 + step, "obs", peer,
            )

        await_bytes(grs.at[step, pl.ds(draws, (n_obs - 1) * draws)], recv_sem.at[7 + step])
        total = gp[step, rows_at(o * draws, draws), :].astype(F32)
        for q in range(1, n_obs):
            total += grs[step, pl.ds(q * draws, draws), :].astype(F32)
        return total

    weights = residual / divisor
    share_weights(0, weights)
    own_m = pltpu.make_async_copy(mrow.at[pl.ds(0, share)], mixed.at[rows_at(t * share, share)], local_sem.at[5])
    own_m.start()

    @pl.loop(1, n_tm)
    def _(r):
        send(mrow.at[rows_at(r * share, share)], mixed.at[rows_at(t * share, share)], 3, "tm", tm_source(r))

    for step in range(SWEEPS):
        total = weighted(step, f_v)
        here = gall.at[step, rows_at(o * draws, draws)]
        gall[step, rows_at(o * draws, draws), :] = total.astype(BF16)

        @pl.loop(1, n_obs)
        def _(q):
            send(here, here, 10 + step, "obs", obs_peer(q))

        if step == 0:
            own_m.wait()
            await_bytes(mixed.at[pl.ds(share, rows - share)], recv_sem.at[3])
        await_bytes(gall.at[step, pl.ds(draws, (n_obs - 1) * draws)], recv_sem.at[10 + step])
        ysend[step] = dot_nt(mixed[...], gall[step]).astype(BF16)

        @pl.loop(1, n_tm)
        def _(r):
            peer = tm_peer(r)
            send(
                ysend.at[step, rows_at(peer * share, share)], yrow.at[step, rows_at(r * share, share)],
                12 + step, "tm", peer,
            )

        await_bytes(yrow.at[step, pl.ds(share, rows - share)], recv_sem.at[12 + step])
        product = ysend[step, rows_at(t * share, share), :].astype(F32)
        product += yrow[step, pl.ds(share, rows - share), :].astype(F32).reshape(n_tm - 1, share, -1).sum(axis=0)
        weights = weights + (residual - product - error * weights) / divisor
        share_weights(step + 1, weights)

    w_ref[...] = weights
    u_ref[...] = weighted(SWEEPS, mixed)

    await_bytes(dall.at[pl.ds(0, (n_obs - 1) * draws)], send_sem.at[0])
    await_bytes(frow.at[pl.ds(share, rows - share)], send_sem.at[1])
    await_bytes(psend.at[pl.ds(share, rows - share)], send_sem.at[2])
    await_bytes(mrow.at[pl.ds(share, rows - share)], send_sem.at[3])
    for step in range(SWEEPS + 1):
        await_bytes(wall.at[step, pl.ds(share, rows - share)], send_sem.at[4 + step])
        await_bytes(gp.at[step, pl.ds(draws, (n_obs - 1) * draws)], send_sem.at[7 + step])
    for step in range(SWEEPS):
        await_bytes(gall.at[step, pl.ds(draws, (n_obs - 1) * draws)], send_sem.at[10 + step])
        await_bytes(ysend.at[step, pl.ds(share, rows - share)], send_sem.at[12 + step])


def body(n_obs, n_tm, footprints, spatial_cov, time_cov, flux_draws, perturbed, obs_error):
    rows, _, cells = footprints.shape
    own_draws = flux_draws.shape[0]
    draws = own_draws * n_obs
    share = rows // n_tm
    any_space = pl.BlockSpec(memory_space=pl.ANY)
    vmem = pl.BlockSpec(memory_space=pltpu.VMEM)
    weights, update = pl.pallas_call(
        functools.partial(kernel, n_obs, n_tm),
        out_shape=(
            jax.ShapeDtypeStruct((share, draws), F32),
            jax.ShapeDtypeStruct((own_draws, cells), F32),
        ),
        in_specs=[any_space, any_space, vmem, any_space, any_space, vmem],
        out_specs=(vmem, vmem),
        scratch_shapes=[
            pltpu.VMEM((rows, cells), BF16),
            pltpu.VMEM((cells, cells), BF16),
            pltpu.VMEM((rows, cells), BF16),
            pltpu.VMEM((rows, cells), BF16),
            pltpu.VMEM((rows, cells), BF16),
            pltpu.VMEM((rows, cells), BF16),
            pltpu.VMEM((draws, cells), BF16),
            pltpu.VMEM((rows, draws), F32),
            pltpu.VMEM((rows, draws), F32),
            pltpu.VMEM((SWEEPS + 1, rows, draws), BF16),
            pltpu.VMEM((draws, rows), BF16),
            pltpu.VMEM((SWEEPS + 1, draws, cells), BF16),
            pltpu.VMEM((SWEEPS + 1, draws, cells), BF16),
            pltpu.VMEM((SWEEPS, draws, cells), BF16),
            pltpu.VMEM((SWEEPS, rows, draws), BF16),
            pltpu.VMEM((SWEEPS, rows, draws), BF16),
            pltpu.VMEM((rows, rows), BF16),
            pltpu.VMEM((rows, rows), BF16),
            pltpu.VMEM((share, draws), F32),
            pltpu.VMEM((share, TILE), F32),
            pltpu.SemaphoreType.DMA((6,)),
            pltpu.SemaphoreType.DMA((14,)),
            pltpu.SemaphoreType.DMA((14,)),
            pltpu.SemaphoreType.DMA((BATCHES,)),
        ],
        compiler_params=pltpu.CompilerParams(
            collective_id=0, has_side_effects=True, vmem_limit_bytes=56 * 1024 * 1024
        ),
    )(
        footprints[:, 0, :], spatial_cov, time_cov, flux_draws[:, 0, :],
        perturbed, obs_error[None, :],
    )
    return weights, update[:, None, :]


def solution(mesh):
    n_obs, n_tm = mesh.shape["obs"], mesh.shape["tm"]
    in_specs = (P("obs", "tm", None), P(), P(), P("obs", "tm", None), P("obs", None), P("obs"))
    out_specs = (P(("obs", "tm"), None), P("obs", "tm", None))
    return jax.shard_map(
        functools.partial(body, n_obs, n_tm), mesh=mesh, in_specs=in_specs, out_specs=out_specs, check_vma=False
    )
```

```python
import functools

import jax
import jax.numpy as jnp
from jax import lax
from jax.experimental import pallas as pl
from jax.experimental.pallas import tpu as pltpu
from jax.sharding import PartitionSpec as P

SWEEPS = 2
MESH = pl.DeviceIdType.MESH
BF16 = jnp.bfloat16
F32 = jnp.float32
TILE = 512
PIECES = 2
HALVES = 2
DRAWS_Z, DRAWS_Y, FOOT, PRED, MIXED = range(5)
WEIGHTS = 5
PARTS = WEIGHTS + (SWEEPS + 1) * HALVES
PARTS_Z = PARTS + (SWEEPS + 1) * HALVES
SUMS_Z = PARTS_Z + (SWEEPS + 1) * HALVES
SUMS = SUMS_Z + SWEEPS * HALVES
PRODUCTS = SUMS + SWEEPS * HALVES
EXCHANGES = PRODUCTS + SWEEPS * HALVES
TM_STEPS = (
    (0, 0, 0), (1, 0, 0), (3, 0, 0), (0, 1, 0), (2, 0, 0), (1, 1, 0), (3, 1, 0), (0, 1, 1),
    (2, 1, 0), (1, 0, 1), (3, 0, 1), (2, 0, 1), (1, 1, 1), (3, 1, 1), (2, 1, 1), (0, 0, 1),
)
OBS_STEPS = ((0, 0), (1, 0), (3, 0), (0, 1), (2, 0), (1, 1), (3, 1), (2, 1))


def dot_nt(left, right):
    return lax.dot_general(left, right, (((1,), (1,)), ((), ())), preferred_element_type=F32)


def dot_nn(left, right):
    return jnp.dot(left, right, preferred_element_type=F32)


def rows_at(start, size):
    return pl.ds(pl.multiple_of(start, size), size)


def kernel(
    n_obs, n_tm,
    f_ref, s_ref, t_ref, d_ref, p_ref, e_ref,
    w_ref, u_ref,
    f_v, s_v, frow, mrow, mixed, dall, psend, prow,
    wall, wt, gp, grs, gz_send, gz, gall, ysend, yrow, mixer, pert, dacc,
    local_sem, send_sem, recv_sem, frecv_sem,
):
    o = lax.axis_index("obs")
    t = lax.axis_index("tm")
    rows, cells = f_ref.shape
    share = rows // n_tm
    draws = d_ref.shape[0]
    part = share // PIECES
    piece_rows = rows // PIECES
    half = draws * n_obs // HALVES
    owned = half // n_obs
    x, z_far, core = t // 4, lax.rem(t // 2, 2), lax.rem(t, 2)
    z_near, y = o // 4, lax.rem(o, 4)

    def tm_at(dx, dz, dc):
        return lax.rem(x + dx, 4) * 4 + lax.rem(z_far + dz, 2) * 2 + lax.rem(core + dc, 2)

    def obs_at(dy, dz):
        return lax.rem(z_near + dz, 2) * 4 + lax.rem(y + dy, 4)

    tm_to = [tm_at(*step) for step in TM_STEPS]
    tm_from = [tm_at(4 - dx, dz, dc) for dx, dz, dc in TM_STEPS]
    obs_to = [obs_at(*step) for step in OBS_STEPS]
    own_share = rows_at(t * share, share)

    unsent = []

    def send(src, dst, phase, axis, peer, recv=None):
        pltpu.make_async_remote_copy(
            src_ref=src, dst_ref=dst, send_sem=send_sem.at[phase],
            recv_sem=recv_sem.at[phase] if recv is None else recv,
            device_id={axis: peer}, device_id_type=MESH,
        ).start()

    def await_bytes(region, sem):
        pltpu.make_async_copy(region, region, sem).wait()

    def sent_later(region, phase):
        unsent.append((region, send_sem.at[phase]))

    load_s = pltpu.make_async_copy(s_ref, s_v, local_sem.at[0])
    load_f = pltpu.make_async_copy(f_ref, f_v, local_sem.at[1])
    load_p = pltpu.make_async_copy(p_ref.at[own_share], pert, local_sem.at[2])
    own_f = [
        pltpu.make_async_copy(
            f_ref.at[rows_at(t * share + piece * part, part)],
            frow.at[pl.ds(piece * piece_rows, part)], local_sem.at[5 + piece],
        )
        for piece in range(PIECES)
    ]

    def half_rows(h, owner):
        return rows_at(h * half + owner * owned, owned)

    own_d = [
        pltpu.make_async_copy(d_ref.at[pl.ds(h * owned, owned)], dall.at[half_rows(h, o)], local_sem.at[(4, 9)[h]])
        for h in range(HALVES)
    ]

    barrier = pltpu.get_barrier_semaphore()
    for peer in tm_to[1:]:
        pl.semaphore_signal(barrier, inc=1, device_id={"tm": peer}, device_id_type=MESH)
    for peer in obs_to[1:]:
        pl.semaphore_signal(barrier, inc=1, device_id={"obs": peer}, device_id_type=MESH)

    load_f.start()
    for copy in own_f:
        copy.start()
    for copy in own_d:
        copy.start()
    load_p.start()
    load_s.start()
    pl.semaphore_wait(barrier, n_tm - 1 + n_obs - 1)

    z_peer = obs_at(0, 1)
    for h in range(HALVES):
        send(d_ref.at[pl.ds(h * owned, owned)], dall.at[half_rows(h, o)], DRAWS_Z, "obs", z_peer)
    sent_later(dall.at[pl.ds(0, draws)], DRAWS_Z)
    for piece in range(PIECES):
        for r in range(1, n_tm):
            send(
                f_ref.at[rows_at(tm_to[r] * share + piece * part, part)],
                frow.at[pl.ds(piece * piece_rows + r * part, part)],
                FOOT, "tm", tm_to[r], frecv_sem.at[piece],
            )
    sent_later(frow.at[pl.ds(share, rows - share)], FOOT)
    for dy in range(1, 4):
        for h in range(HALVES):
            send(d_ref.at[pl.ds(h * owned, owned)], dall.at[half_rows(h, o)], DRAWS_Y, "obs", obs_at(dy, 0))
    await_bytes(dall.at[pl.ds(0, draws)], recv_sem.at[DRAWS_Z])
    for dy in range(1, 4):
        for h in range(HALVES):
            here = dall.at[half_rows(h, z_peer)]
            send(here, here, DRAWS_Y, "obs", obs_at(dy, 0))
    sent_later(dall.at[pl.ds(0, 6 * draws)], DRAWS_Y)

    def periods(shape, dim):
        slot = lax.broadcasted_iota(jnp.int32, shape, dim) // part
        period = jnp.zeros(shape, jnp.int32)
        for r in range(n_tm):
            period = jnp.where(slot == r, tm_from[r], period)
        return period

    pick = (periods((piece_rows, n_tm), 0) == lax.broadcasted_iota(jnp.int32, (piece_rows, n_tm), 1)).astype(F32)
    pick_t = (periods((n_tm, piece_rows), 1) == lax.broadcasted_iota(jnp.int32, (n_tm, piece_rows), 0)).astype(F32)
    picked = jnp.dot(t_ref[...], pick_t, precision=lax.Precision.HIGHEST, preferred_element_type=F32)
    full = jnp.dot(pick, picked, precision=lax.Precision.HIGHEST, preferred_element_type=F32)
    row_in = lax.rem(lax.broadcasted_iota(jnp.int32, (piece_rows, piece_rows), 0), part)
    col_in = lax.rem(lax.broadcasted_iota(jnp.int32, (piece_rows, piece_rows), 1), part)
    full = jnp.where(row_in == col_in, full, 0.0)
    high = full.astype(BF16)
    mixer[pl.ds(0, piece_rows), :] = high
    mixer[pl.ds(piece_rows, piece_rows), :] = (full - high.astype(F32)).astype(BF16)
    dacc[...] = jnp.zeros_like(dacc)

    load_f.wait()
    for copy in own_d:
        copy.wait()
    await_bytes(dall.at[pl.ds(0, 6 * draws)], recv_sem.at[DRAWS_Y])
    psend[...] = dot_nt(f_v[...], dall[...])
    for r in range(1, n_tm):
        send(psend.at[rows_at(tm_to[r] * share, share)], prow.at[pl.ds(r * share, share)], PRED, "tm", tm_to[r])
    sent_later(psend.at[pl.ds(share, rows - share)], PRED)

    def send_mixed(piece):
        pltpu.make_async_copy(
            mrow.at[pl.ds(piece * piece_rows, part)],
            mixed.at[rows_at(t * share + piece * part, part)], local_sem.at[7 + piece],
        ).start()
        for r in range(1, n_tm):
            send(
                mrow.at[pl.ds(piece * piece_rows + r * part, part)],
                mixed.at[rows_at(t * share + piece * part, part)], MIXED, "tm", tm_from[r],
            )

    load_s.wait()
    for piece in range(PIECES):
        own_f[piece].wait()
        await_bytes(frow.at[pl.ds(piece * piece_rows + part, piece_rows - part)], frecv_sem.at[piece])
        here = pl.ds(piece * piece_rows, piece_rows)

        @pl.loop(0, cells // TILE)
        def _(c):
            cols = pl.ds(pl.multiple_of(c * TILE, TILE), TILE)
            block = dot_nn(frow[here, :], s_v[:, cols]).astype(BF16)
            both = dot_nn(mixer[...], block)
            out = (both[:piece_rows] + both[piece_rows:]).astype(BF16)
            mrow[here, cols] = out
            product = out.astype(F32) * frow[here, cols].astype(F32)
            dacc[pl.ds(piece * part, part), :] += product.reshape(n_tm, part, TILE).sum(axis=0)

        if piece < PIECES - 1:
            send_mixed(piece)

    load_p.wait()
    await_bytes(prow.at[pl.ds(share, rows - share)], recv_sem.at[PRED])
    predicted = psend[own_share, :]
    predicted += prow[pl.ds(share, rows - share), :].reshape(n_tm - 1, share, -1).sum(axis=0)
    at_row = lax.broadcasted_iota(jnp.int32, (share, rows), 0) + t * share
    at_col = lax.broadcasted_iota(jnp.int32, (share, rows), 1)
    error = jnp.where(at_row == at_col, jnp.broadcast_to(e_ref[...], (share, rows)), 0.0).sum(axis=1, keepdims=True)
    divisor = dacc[...].sum(axis=1, keepdims=True) + error
    column = lax.broadcasted_iota(jnp.int32, (n_obs * draws, n_obs * draws), 1)
    in_half = lax.rem(column, half)
    draw = in_half // owned * draws + column // half * owned + lax.rem(column, owned)
    order = (lax.broadcasted_iota(jnp.int32, column.shape, 0) == draw).astype(F32)
    ordered = jnp.dot(pert[...], order, precision=lax.Precision.HIGHEST, preferred_element_type=F32)
    whole = ordered - predicted
    residual = [whole[:, h * half:(h + 1) * half] for h in range(HALVES)]

    def send_weights(step, h, weights):
        wall[step, h, own_share, :] = weights.astype(BF16)
        here = wall.at[step, h, own_share]
        phase = WEIGHTS + step * HALVES + h
        for r in range(1, n_tm):
            send(here, here, phase, "tm", tm_to[r])
        sent_later(wall.at[step, h, pl.ds(share, rows - share)], phase)

    def receive_weights(step, h):
        await_bytes(wall.at[step, h, pl.ds(share, rows - share)], recv_sem.at[WEIGHTS + step * HALVES + h])
        wt[pl.ds(h * half, half), :] = wall[step, h].T

    def back_project(step, h):
        receive_weights(step, h)

        source = f_v if step < SWEEPS else mixed
        gp[step, h] = dot_nn(wt[pl.ds(h * half, half), :], source[...]).astype(BF16)
        phase = PARTS + step * HALVES + h
        for dz in range(2):
            for dy in range(1, 4):
                send(
                    gp.at[step, h, rows_at(obs_at(dy, 1 - dz) * owned, owned)],
                    grs.at[step, h, pl.ds(((1 - dz) * 3 + dy - 1) * owned, owned)], phase, "obs", obs_at(dy, 0),
                )
        sent_later(grs.at[step, h], phase)

    def line_sum(step, h, dz):
        total = gp[step, h, rows_at(obs_at(0, dz) * owned, owned), :].astype(F32)
        for dy in range(3):
            total += grs[step, h, pl.ds((dz * 3 + dy) * owned, owned), :].astype(F32)
        return total

    def pass_parts(step, h):
        await_bytes(grs.at[step, h], recv_sem.at[PARTS + step * HALVES + h])
        gz_send[step, h] = line_sum(step, h, 1).astype(BF16)
        phase = PARTS_Z + step * HALVES + h
        send(gz_send.at[step, h], gz.at[step, h], phase, "obs", z_peer)
        sent_later(gz_send.at[step, h], phase)

    def received_sum(step, h):
        await_bytes(gz.at[step, h], recv_sem.at[PARTS_Z + step * HALVES + h])
        return line_sum(step, h, 0) + gz[step, h].astype(F32)

    def sum_parts(step, h):
        here = gall.at[step, h, rows_at(o * owned, owned)]
        here[...] = received_sum(step, h).astype(BF16)
        send(here, here, SUMS_Z + step * HALVES + h, "obs", z_peer)
        sent_later(here, SUMS_Z + step * HALVES + h)
        for dy in range(1, 4):
            send(here, here, SUMS + step * HALVES + h, "obs", obs_at(dy, 0))

    def pass_sums(step, h):
        here = gall.at[step, h, rows_at(z_peer * owned, owned)]
        await_bytes(here, recv_sem.at[SUMS_Z + step * HALVES + h])
        for dy in range(1, 4):
            send(here, here, SUMS + step * HALVES + h, "obs", obs_at(dy, 0))
        sent_later(grs.at[step, h], SUMS + step * HALVES + h)

    def exchange(step):
        pass_parts(step, 0)
        pass_parts(step, 1)
        sum_parts(step, 0)
        pass_sums(step, 0)
        sum_parts(step, 1)
        pass_sums(step, 1)

    def project(step, h):
        await_bytes(grs.at[step, h], recv_sem.at[SUMS + step * HALVES + h])
        ysend[step, h] = dot_nt(mixed[...], gall[step, h]).astype(BF16)
        phase = PRODUCTS + step * HALVES + h
        for r in range(1, n_tm):
            send(
                ysend.at[step, h, rows_at(tm_to[r] * share, share)],
                yrow.at[step, h, pl.ds(r * share, share)], phase, "tm", tm_to[r],
            )
        sent_later(ysend.at[step, h, pl.ds(share, rows - share)], phase)

    def correct(step, h):
        await_bytes(yrow.at[step, h, pl.ds(share, rows - share)], recv_sem.at[PRODUCTS + step * HALVES + h])
        product = ysend[step, h, own_share, :].astype(F32)
        received = yrow[step, h, pl.ds(share, rows - share), :].astype(F32)
        product += received.reshape(n_tm - 1, share, half).sum(axis=0)
        weights[h] = weights[h] + (residual[h] - product - error * weights[h]) / divisor
        send_weights(step + 1, h, weights[h])

    weights = [residual[h] / divisor for h in range(HALVES)]
    for h in range(HALVES):
        send_weights(0, h, weights[h])
    send_mixed(PIECES - 1)
    sent_later(mrow.at[pl.ds(share, rows - share)], MIXED)

    back_project(0, 0)
    back_project(0, 1)
    exchange(0)
    for piece in range(PIECES):
        pltpu.make_async_copy(
            mrow.at[pl.ds(0, part)], mixed.at[pl.ds(0, part)], local_sem.at[7 + piece]
        ).wait()
    await_bytes(mixed.at[pl.ds(share, rows - share)], recv_sem.at[MIXED])
    for step in range(SWEEPS):
        project(step, 0)
        correct(step, 0)
        project(step, 1)
        back_project(step + 1, 0)
        correct(step, 1)
        back_project(step + 1, 1)
        if step < SWEEPS - 1:
            exchange(step + 1)

    for h in range(HALVES):
        pass_parts(SWEEPS, h)
    last = jnp.concatenate(weights, axis=1)
    w_ref[...] = lax.dot_general(
        last, order, (((1,), (1,)), ((), ())), precision=lax.Precision.HIGHEST, preferred_element_type=F32
    )
    for h in range(HALVES):
        u_ref[pl.ds(h * owned, owned), :] = received_sum(SWEEPS, h)

    for region, sem in unsent:
        await_bytes(region, sem)


def body(n_obs, n_tm, footprints, spatial_cov, time_cov, flux_draws, perturbed, obs_error):
    rows, _, cells = footprints.shape
    own_draws = flux_draws.shape[0]
    draws = own_draws * n_obs
    share = rows // n_tm
    half = draws // HALVES
    any_space = pl.BlockSpec(memory_space=pl.ANY)
    vmem = pl.BlockSpec(memory_space=pltpu.VMEM)
    weights, update = pl.pallas_call(
        functools.partial(kernel, n_obs, n_tm),
        out_shape=(
            jax.ShapeDtypeStruct((share, draws), F32),
            jax.ShapeDtypeStruct((own_draws, cells), F32),
        ),
        in_specs=[any_space, any_space, vmem, any_space, any_space, vmem],
        out_specs=(vmem, vmem),
        scratch_shapes=[
            pltpu.VMEM((rows, cells), BF16),
            pltpu.VMEM((cells, cells), BF16),
            pltpu.VMEM((rows, cells), BF16),
            pltpu.VMEM((rows, cells), BF16),
            pltpu.VMEM((rows, cells), BF16),
            pltpu.VMEM((draws, cells), BF16),
            pltpu.VMEM((rows, draws), F32),
            pltpu.VMEM((rows, draws), F32),
            pltpu.VMEM((SWEEPS + 1, HALVES, rows, half), BF16),
            pltpu.VMEM((draws, rows), BF16),
            pltpu.VMEM((SWEEPS + 1, HALVES, half, cells), BF16),
            pltpu.VMEM((SWEEPS + 1, HALVES, 6 * half // n_obs, cells), BF16),
            pltpu.VMEM((SWEEPS + 1, HALVES, half // n_obs, cells), BF16),
            pltpu.VMEM((SWEEPS + 1, HALVES, half // n_obs, cells), BF16),
            pltpu.VMEM((SWEEPS, HALVES, half, cells), BF16),
            pltpu.VMEM((SWEEPS, HALVES, rows, half), BF16),
            pltpu.VMEM((SWEEPS, HALVES, rows, half), BF16),
            pltpu.VMEM((2 * rows // PIECES, rows // PIECES), BF16),
            pltpu.VMEM((share, draws), F32),
            pltpu.VMEM((share, TILE), F32),
            pltpu.SemaphoreType.DMA((10,)),
            pltpu.SemaphoreType.DMA((EXCHANGES,)),
            pltpu.SemaphoreType.DMA((EXCHANGES,)),
            pltpu.SemaphoreType.DMA((PIECES,)),
        ],
        compiler_params=pltpu.CompilerParams(
            collective_id=0, has_side_effects=True, vmem_limit_bytes=56 * 1024 * 1024
        ),
    )(
        footprints[:, 0, :], spatial_cov, time_cov, flux_draws[:, 0, :],
        perturbed, obs_error[None, :],
    )
    return weights, update[:, None, :]


def solution(mesh):
    n_obs, n_tm = mesh.shape["obs"], mesh.shape["tm"]
    in_specs = (P("obs", "tm", None), P(), P(), P("obs", "tm", None), P("obs", None), P("obs"))
    out_specs = (P(("obs", "tm"), None), P("obs", "tm", None))
    return jax.shard_map(
        functools.partial(body, n_obs, n_tm), mesh=mesh, in_specs=in_specs, out_specs=out_specs, check_vma=False
    )
```

```python
import functools

import jax
import jax.numpy as jnp
from jax import lax
from jax.experimental import pallas as pl
from jax.experimental.pallas import tpu as pltpu
from jax.sharding import PartitionSpec as P

SWEEPS = 2
MESH = pl.DeviceIdType.MESH
BF16 = jnp.bfloat16
F32 = jnp.float32
TILE = 512
PIECES = 2
HALVES = 2
STAGED = (True, False, False)
DRAWS_Z, DRAWS_Y, FOOT, PRED, MIXED = range(5)
WEIGHTS = 5
PARTS = WEIGHTS + (SWEEPS + 1) * HALVES
PARTS_Z = PARTS + (SWEEPS + 1) * HALVES
SUMS_Z = PARTS_Z + (SWEEPS + 1) * HALVES
SUMS = SUMS_Z + SWEEPS * HALVES
PRODUCTS = SUMS + SWEEPS * HALVES
EXCHANGES = PRODUCTS + SWEEPS * HALVES
TM_STEPS = (
    (0, 0, 0), (1, 0, 0), (3, 0, 0), (0, 1, 0), (2, 0, 0), (1, 1, 0), (3, 1, 0), (0, 1, 1),
    (2, 1, 0), (1, 0, 1), (3, 0, 1), (2, 0, 1), (1, 1, 1), (3, 1, 1), (2, 1, 1), (0, 0, 1),
)
OBS_STEPS = ((0, 0), (1, 0), (3, 0), (0, 1), (2, 0), (1, 1), (3, 1), (2, 1))


def dot_nt(left, right):
    return lax.dot_general(left, right, (((1,), (1,)), ((), ())), preferred_element_type=F32)


def dot_nn(left, right):
    return jnp.dot(left, right, preferred_element_type=F32)


def rows_at(start, size):
    return pl.ds(pl.multiple_of(start, size), size)


def kernel(
    n_obs, n_tm,
    f_ref, s_ref, t_ref, d_ref, p_ref, e_ref,
    w_ref, u_ref,
    f_v, s_v, frow, mrow, mixed, dall, psend, prow,
    wall, wt, gp, grs, gz_send, gz, gall, ysend, yrow, mixer, pert, dacc,
    local_sem, send_sem, recv_sem, frecv_sem,
):
    o = lax.axis_index("obs")
    t = lax.axis_index("tm")
    rows, cells = f_ref.shape
    share = rows // n_tm
    draws = d_ref.shape[0]
    part = share // PIECES
    piece_rows = rows // PIECES
    half = draws * n_obs // HALVES
    owned = half // n_obs
    x, z_far, core = t // 4, lax.rem(t // 2, 2), lax.rem(t, 2)
    z_near, y = o // 4, lax.rem(o, 4)

    def tm_at(dx, dz, dc):
        return lax.rem(x + dx, 4) * 4 + lax.rem(z_far + dz, 2) * 2 + lax.rem(core + dc, 2)

    def obs_at(dy, dz):
        return lax.rem(z_near + dz, 2) * 4 + lax.rem(y + dy, 4)

    tm_to = [tm_at(*step) for step in TM_STEPS]
    tm_from = [tm_at(4 - dx, dz, dc) for dx, dz, dc in TM_STEPS]
    obs_to = [obs_at(*step) for step in OBS_STEPS]
    own_share = rows_at(t * share, share)

    unsent = []

    def send(src, dst, phase, axis, peer, recv=None):
        pltpu.make_async_remote_copy(
            src_ref=src, dst_ref=dst, send_sem=send_sem.at[phase],
            recv_sem=recv_sem.at[phase] if recv is None else recv,
            device_id={axis: peer}, device_id_type=MESH,
        ).start()

    def await_bytes(region, sem):
        pltpu.make_async_copy(region, region, sem).wait()

    def sent_later(region, phase):
        unsent.append((region, send_sem.at[phase]))

    load_s = pltpu.make_async_copy(s_ref, s_v, local_sem.at[0])
    load_f = pltpu.make_async_copy(f_ref, f_v, local_sem.at[1])
    load_p = pltpu.make_async_copy(p_ref.at[own_share], pert, local_sem.at[2])
    own_f = [
        pltpu.make_async_copy(
            f_ref.at[rows_at(t * share + piece * part, part)],
            frow.at[pl.ds(piece * piece_rows, part)], local_sem.at[5 + piece],
        )
        for piece in range(PIECES)
    ]

    def half_rows(h, owner):
        return rows_at(h * half + owner * owned, owned)

    own_d = [
        pltpu.make_async_copy(d_ref.at[pl.ds(h * owned, owned)], dall.at[half_rows(h, o)], local_sem.at[(4, 9)[h]])
        for h in range(HALVES)
    ]

    barrier = pltpu.get_barrier_semaphore()
    for peer in tm_to[1:]:
        pl.semaphore_signal(barrier, inc=1, device_id={"tm": peer}, device_id_type=MESH)
    for peer in obs_to[1:]:
        pl.semaphore_signal(barrier, inc=1, device_id={"obs": peer}, device_id_type=MESH)

    load_f.start()
    for copy in own_f:
        copy.start()
    for copy in own_d:
        copy.start()
    load_p.start()
    load_s.start()
    pl.semaphore_wait(barrier, n_tm - 1 + n_obs - 1)

    z_peer = obs_at(0, 1)
    for h in range(HALVES):
        send(d_ref.at[pl.ds(h * owned, owned)], dall.at[half_rows(h, o)], DRAWS_Z, "obs", z_peer)
    sent_later(dall.at[pl.ds(0, draws)], DRAWS_Z)
    def send_footprints(piece):
        for r in range(1, n_tm):
            send(
                f_ref.at[rows_at(tm_to[r] * share + piece * part, part)],
                frow.at[pl.ds(piece * piece_rows + r * part, part)],
                FOOT, "tm", tm_to[r], frecv_sem.at[piece],
            )

    send_footprints(0)
    sent_later(frow.at[pl.ds(share, rows - share)], FOOT)
    for dy in range(1, 4):
        for h in range(HALVES):
            send(d_ref.at[pl.ds(h * owned, owned)], dall.at[half_rows(h, o)], DRAWS_Y, "obs", obs_at(dy, 0))
    await_bytes(dall.at[pl.ds(0, draws)], recv_sem.at[DRAWS_Z])
    for dy in range(1, 4):
        for h in range(HALVES):
            here = dall.at[half_rows(h, z_peer)]
            send(here, here, DRAWS_Y, "obs", obs_at(dy, 0))
    sent_later(dall.at[pl.ds(0, 6 * draws)], DRAWS_Y)

    load_f.wait()
    for copy in own_d:
        copy.wait()
    await_bytes(dall.at[pl.ds(0, 6 * draws)], recv_sem.at[DRAWS_Y])
    psend[...] = dot_nt(f_v[...], dall[...])
    for r in range(1, n_tm):
        send(psend.at[rows_at(tm_to[r] * share, share)], prow.at[pl.ds(r * share, share)], PRED, "tm", tm_to[r])
    sent_later(psend.at[pl.ds(share, rows - share)], PRED)
    for piece in range(1, PIECES):
        send_footprints(piece)

    def periods(shape, dim):
        slot = lax.broadcasted_iota(jnp.int32, shape, dim) // part
        period = jnp.zeros(shape, jnp.int32)
        for r in range(n_tm):
            period = jnp.where(slot == r, tm_from[r], period)
        return period

    pick = (periods((piece_rows, n_tm), 0) == lax.broadcasted_iota(jnp.int32, (piece_rows, n_tm), 1)).astype(F32)
    pick_t = (periods((n_tm, piece_rows), 1) == lax.broadcasted_iota(jnp.int32, (n_tm, piece_rows), 0)).astype(F32)
    picked = jnp.dot(t_ref[...], pick_t, precision=lax.Precision.HIGHEST, preferred_element_type=F32)
    full = jnp.dot(pick, picked, precision=lax.Precision.HIGHEST, preferred_element_type=F32)
    row_in = lax.rem(lax.broadcasted_iota(jnp.int32, (piece_rows, piece_rows), 0), part)
    col_in = lax.rem(lax.broadcasted_iota(jnp.int32, (piece_rows, piece_rows), 1), part)
    full = jnp.where(row_in == col_in, full, 0.0)
    high = full.astype(BF16)
    mixer[pl.ds(0, piece_rows), :] = high
    mixer[pl.ds(piece_rows, piece_rows), :] = (full - high.astype(F32)).astype(BF16)
    dacc[...] = jnp.zeros_like(dacc)

    def send_mixed(piece):
        pltpu.make_async_copy(
            mrow.at[pl.ds(piece * piece_rows, part)],
            mixed.at[rows_at(t * share + piece * part, part)], local_sem.at[7 + piece],
        ).start()
        for r in range(1, n_tm):
            send(
                mrow.at[pl.ds(piece * piece_rows + r * part, part)],
                mixed.at[rows_at(t * share + piece * part, part)], MIXED, "tm", tm_from[r],
            )

    load_s.wait()
    for piece in range(PIECES):
        own_f[piece].wait()
        await_bytes(frow.at[pl.ds(piece * piece_rows + part, piece_rows - part)], frecv_sem.at[piece])
        here = pl.ds(piece * piece_rows, piece_rows)

        @pl.loop(0, cells // TILE)
        def _(c):
            cols = pl.ds(pl.multiple_of(c * TILE, TILE), TILE)
            block = dot_nn(frow[here, :], s_v[:, cols]).astype(BF16)
            both = dot_nn(mixer[...], block)
            out = (both[:piece_rows] + both[piece_rows:]).astype(BF16)
            mrow[here, cols] = out
            product = out.astype(F32) * frow[here, cols].astype(F32)
            dacc[pl.ds(piece * part, part), :] += product.reshape(n_tm, part, TILE).sum(axis=0)

    load_p.wait()
    await_bytes(prow.at[pl.ds(share, rows - share)], recv_sem.at[PRED])
    predicted = psend[own_share, :]
    predicted += prow[pl.ds(share, rows - share), :].reshape(n_tm - 1, share, -1).sum(axis=0)
    at_row = lax.broadcasted_iota(jnp.int32, (share, rows), 0) + t * share
    at_col = lax.broadcasted_iota(jnp.int32, (share, rows), 1)
    error = jnp.where(at_row == at_col, jnp.broadcast_to(e_ref[...], (share, rows)), 0.0).sum(axis=1, keepdims=True)
    divisor = dacc[...].sum(axis=1, keepdims=True) + error
    column = lax.broadcasted_iota(jnp.int32, (n_obs * draws, n_obs * draws), 1)
    in_half = lax.rem(column, half)
    draw = in_half // owned * draws + column // half * owned + lax.rem(column, owned)
    order = (lax.broadcasted_iota(jnp.int32, column.shape, 0) == draw).astype(F32)
    ordered = jnp.dot(pert[...], order, precision=lax.Precision.HIGHEST, preferred_element_type=F32)
    whole = ordered - predicted
    residual = [whole[:, h * half:(h + 1) * half] for h in range(HALVES)]

    def send_weights(step, h, weights):
        wall[step, h, own_share, :] = weights.astype(BF16)
        here = wall.at[step, h, own_share]
        phase = WEIGHTS + step * HALVES + h
        for r in range(1, n_tm):
            send(here, here, phase, "tm", tm_to[r])
        sent_later(wall.at[step, h, pl.ds(share, rows - share)], phase)

    def receive_weights(step, h):
        await_bytes(wall.at[step, h, pl.ds(share, rows - share)], recv_sem.at[WEIGHTS + step * HALVES + h])
        wt[pl.ds(h * half, half), :] = wall[step, h].T

    def targets(step):
        if STAGED[step]:
            return [(dy, dz) for dz in (1, 0) for dy in (1, 3, 2)]
        return OBS_STEPS[1:]

    def back_project(step, h):
        receive_weights(step, h)

        source = f_v if step < SWEEPS else mixed
        gp[step, h] = dot_nn(wt[pl.ds(h * half, half), :], source[...]).astype(BF16)
        phase = PARTS + step * HALVES + h
        for slot, (dy, dz) in enumerate(targets(step)):
            send(
                gp.at[step, h, rows_at(obs_at(dy, dz) * owned, owned)],
                grs.at[step, h, pl.ds(slot * owned, owned)], phase, "obs",
                obs_at(dy, 0) if STAGED[step] else obs_at(dy, dz),
            )
        sent_later(grs.at[step, h, pl.ds(0, len(targets(step)) * owned)], phase)

    def line_sum(step, h, dz):
        total = gp[step, h, rows_at(obs_at(0, dz) * owned, owned), :].astype(F32)
        for slot, target in enumerate(targets(step)):
            if not STAGED[step] or target[1] == dz:
                total += grs[step, h, pl.ds(slot * owned, owned), :].astype(F32)
        return total

    def await_parts(step, h):
        await_bytes(grs.at[step, h, pl.ds(0, len(targets(step)) * owned)], recv_sem.at[PARTS + step * HALVES + h])

    def pass_parts(step, h):
        if not STAGED[step]:
            return
        await_parts(step, h)
        gz_send[step, h] = line_sum(step, h, 1).astype(BF16)
        phase = PARTS_Z + step * HALVES + h
        send(gz_send.at[step, h], gz.at[step, h], phase, "obs", z_peer)
        sent_later(gz_send.at[step, h], phase)

    def received_sum(step, h):
        if not STAGED[step]:
            await_parts(step, h)
            return line_sum(step, h, 0)
        await_bytes(gz.at[step, h], recv_sem.at[PARTS_Z + step * HALVES + h])
        return line_sum(step, h, 0) + gz[step, h].astype(F32)

    def sum_parts(step, h):
        here = gall.at[step, h, rows_at(o * owned, owned)]
        here[...] = received_sum(step, h).astype(BF16)
        phase = SUMS + step * HALVES + h
        if STAGED[step]:
            send(here, here, SUMS_Z + step * HALVES + h, "obs", z_peer)
            sent_later(here, SUMS_Z + step * HALVES + h)
            for dy in (1, 3, 2):
                send(here, here, phase, "obs", obs_at(dy, 0))
        else:
            for peer in obs_to[1:]:
                send(here, here, phase, "obs", peer)
        sent_later(grs.at[step, h, pl.ds(0, len(targets(step)) * owned)], phase)

    def pass_sums(step, h):
        if not STAGED[step]:
            return
        here = gall.at[step, h, rows_at(z_peer * owned, owned)]
        await_bytes(here, recv_sem.at[SUMS_Z + step * HALVES + h])
        for dy in (1, 3, 2):
            send(here, here, SUMS + step * HALVES + h, "obs", obs_at(dy, 0))

    def exchange(step):
        pass_parts(step, 0)
        pass_parts(step, 1)
        sum_parts(step, 0)
        pass_sums(step, 0)
        sum_parts(step, 1)
        pass_sums(step, 1)

    def project(step, h):
        await_bytes(grs.at[step, h, pl.ds(0, len(targets(step)) * owned)], recv_sem.at[SUMS + step * HALVES + h])
        ysend[step, h] = dot_nt(mixed[...], gall[step, h]).astype(BF16)
        phase = PRODUCTS + step * HALVES + h
        for r in range(1, n_tm):
            send(
                ysend.at[step, h, rows_at(tm_to[r] * share, share)],
                yrow.at[step, h, pl.ds(r * share, share)], phase, "tm", tm_to[r],
            )
        sent_later(ysend.at[step, h, pl.ds(share, rows - share)], phase)

    def correct(step, h):
        await_bytes(yrow.at[step, h, pl.ds(share, rows - share)], recv_sem.at[PRODUCTS + step * HALVES + h])
        product = ysend[step, h, own_share, :].astype(F32)
        received = yrow[step, h, pl.ds(share, rows - share), :].astype(F32)
        product += received.reshape(n_tm - 1, share, half).sum(axis=0)
        weights[h] = weights[h] + (residual[h] - product - error * weights[h]) / divisor
        send_weights(step + 1, h, weights[h])

    weights = [residual[h] / divisor for h in range(HALVES)]
    for h in range(HALVES):
        send_weights(0, h, weights[h])
    send_mixed(0)
    sent_later(mrow.at[pl.ds(share, rows - share)], MIXED)

    back_project(0, 0)
    back_project(0, 1)
    send_mixed(1)
    exchange(0)
    for piece in range(PIECES):
        pltpu.make_async_copy(
            mrow.at[pl.ds(0, part)], mixed.at[pl.ds(0, part)], local_sem.at[7 + piece]
        ).wait()
    await_bytes(mixed.at[pl.ds(share, rows - share)], recv_sem.at[MIXED])
    for step in range(SWEEPS):
        project(step, 0)
        project(step, 1)
        correct(step, 0)
        correct(step, 1)
        back_project(step + 1, 0)
        back_project(step + 1, 1)
        if step < SWEEPS - 1:
            exchange(step + 1)

    for h in range(HALVES):
        pass_parts(SWEEPS, h)
    last = jnp.concatenate(weights, axis=1)
    w_ref[...] = lax.dot_general(
        last, order, (((1,), (1,)), ((), ())), precision=lax.Precision.HIGHEST, preferred_element_type=F32
    )
    for h in range(HALVES):
        u_ref[pl.ds(h * owned, owned), :] = received_sum(SWEEPS, h)

    for region, sem in unsent:
        await_bytes(region, sem)


def body(n_obs, n_tm, footprints, spatial_cov, time_cov, flux_draws, perturbed, obs_error):
    rows, _, cells = footprints.shape
    own_draws = flux_draws.shape[0]
    draws = own_draws * n_obs
    share = rows // n_tm
    half = draws // HALVES
    any_space = pl.BlockSpec(memory_space=pl.ANY)
    vmem = pl.BlockSpec(memory_space=pltpu.VMEM)
    weights, update = pl.pallas_call(
        functools.partial(kernel, n_obs, n_tm),
        out_shape=(
            jax.ShapeDtypeStruct((share, draws), F32),
            jax.ShapeDtypeStruct((own_draws, cells), F32),
        ),
        in_specs=[any_space, any_space, vmem, any_space, any_space, vmem],
        out_specs=(vmem, vmem),
        scratch_shapes=[
            pltpu.VMEM((rows, cells), BF16),
            pltpu.VMEM((cells, cells), BF16),
            pltpu.VMEM((rows, cells), BF16),
            pltpu.VMEM((rows, cells), BF16),
            pltpu.VMEM((rows, cells), BF16),
            pltpu.VMEM((draws, cells), BF16),
            pltpu.VMEM((rows, draws), F32),
            pltpu.VMEM((rows, draws), F32),
            pltpu.VMEM((SWEEPS + 1, HALVES, rows, half), BF16),
            pltpu.VMEM((draws, rows), BF16),
            pltpu.VMEM((SWEEPS + 1, HALVES, half, cells), BF16),
            pltpu.VMEM((SWEEPS + 1, HALVES, 7 * half // n_obs, cells), BF16),
            pltpu.VMEM((SWEEPS + 1, HALVES, half // n_obs, cells), BF16),
            pltpu.VMEM((SWEEPS + 1, HALVES, half // n_obs, cells), BF16),
            pltpu.VMEM((SWEEPS, HALVES, half, cells), BF16),
            pltpu.VMEM((SWEEPS, HALVES, rows, half), BF16),
            pltpu.VMEM((SWEEPS, HALVES, rows, half), BF16),
            pltpu.VMEM((2 * rows // PIECES, rows // PIECES), BF16),
            pltpu.VMEM((share, draws), F32),
            pltpu.VMEM((share, TILE), F32),
            pltpu.SemaphoreType.DMA((10,)),
            pltpu.SemaphoreType.DMA((EXCHANGES,)),
            pltpu.SemaphoreType.DMA((EXCHANGES,)),
            pltpu.SemaphoreType.DMA((PIECES,)),
        ],
        compiler_params=pltpu.CompilerParams(
            collective_id=0, has_side_effects=True, vmem_limit_bytes=56 * 1024 * 1024
        ),
    )(
        footprints[:, 0, :], spatial_cov, time_cov, flux_draws[:, 0, :],
        perturbed, obs_error[None, :],
    )
    return weights, update[:, None, :]


def solution(mesh):
    n_obs, n_tm = mesh.shape["obs"], mesh.shape["tm"]
    in_specs = (P("obs", "tm", None), P(), P(), P("obs", "tm", None), P("obs", None), P("obs"))
    out_specs = (P(("obs", "tm"), None), P("obs", "tm", None))
    return jax.shard_map(
        functools.partial(body, n_obs, n_tm), mesh=mesh, in_specs=in_specs, out_specs=out_specs, check_vma=False
    )
```

```python
import functools

import jax
import jax.numpy as jnp
from jax import lax
from jax.experimental import pallas as pl
from jax.experimental.pallas import tpu as pltpu
from jax.sharding import PartitionSpec as P

SWEEPS = 2
MESH = pl.DeviceIdType.MESH
BF16 = jnp.bfloat16
F32 = jnp.float32
TILE = 1024
PIECES = 2
HALVES = 2
STAGED = (True, False, False)
DRAWS_Z, DRAWS_Y, FOOT, PRED, MIXED = range(5)
WEIGHTS = 5
PARTS = WEIGHTS + (SWEEPS + 1) * HALVES
PARTS_Z = PARTS + (SWEEPS + 1) * HALVES
SUMS_Z = PARTS_Z + (SWEEPS + 1) * HALVES
SUMS = SUMS_Z + SWEEPS * HALVES
PRODUCTS = SUMS + SWEEPS * HALVES
EXCHANGES = PRODUCTS + SWEEPS * HALVES
TM_STEPS = (
    (0, 0, 0), (1, 0, 0), (3, 0, 0), (0, 1, 0), (2, 0, 0), (1, 1, 0), (3, 1, 0), (0, 1, 1),
    (2, 1, 0), (1, 0, 1), (3, 0, 1), (2, 0, 1), (1, 1, 1), (3, 1, 1), (2, 1, 1), (0, 0, 1),
)
OBS_STEPS = ((0, 0), (1, 0), (3, 0), (0, 1), (2, 0), (1, 1), (3, 1), (2, 1))


def dot_nt(left, right):
    return lax.dot_general(left, right, (((1,), (1,)), ((), ())), preferred_element_type=F32)


def dot_nn(left, right):
    return jnp.dot(left, right, preferred_element_type=F32)


def rows_at(start, size):
    return pl.ds(pl.multiple_of(start, size), size)


def kernel(
    n_obs, n_tm,
    f_ref, s_ref, t_ref, d_ref, p_ref, e_ref,
    w_ref, u_ref,
    f_v, s_v, frow, mrow, mixed, dall, psend, prow,
    wall, wt, gp, grs, gz_send, gz, gall, ysend, yrow, mixer, pert, dacc,
    local_sem, send_sem, recv_sem, frecv_sem,
):
    o = lax.axis_index("obs")
    t = lax.axis_index("tm")
    rows, cells = f_ref.shape
    share = rows // n_tm
    draws = d_ref.shape[0]
    part = share // PIECES
    piece_rows = rows // PIECES
    half = draws * n_obs // HALVES
    owned = half // n_obs
    x, z_far, core = t // 4, lax.rem(t // 2, 2), lax.rem(t, 2)
    z_near, y = o // 4, lax.rem(o, 4)

    def tm_at(dx, dz, dc):
        return lax.rem(x + dx, 4) * 4 + lax.rem(z_far + dz, 2) * 2 + lax.rem(core + dc, 2)

    def obs_at(dy, dz):
        return lax.rem(z_near + dz, 2) * 4 + lax.rem(y + dy, 4)

    tm_to = [tm_at(*step) for step in TM_STEPS]
    tm_from = [tm_at(4 - dx, dz, dc) for dx, dz, dc in TM_STEPS]
    obs_to = [obs_at(*step) for step in OBS_STEPS]
    own_share = rows_at(t * share, share)

    unsent = []

    def send(src, dst, phase, axis, peer, recv=None):
        pltpu.make_async_remote_copy(
            src_ref=src, dst_ref=dst, send_sem=send_sem.at[phase],
            recv_sem=recv_sem.at[phase] if recv is None else recv,
            device_id={axis: peer}, device_id_type=MESH,
        ).start()

    def await_bytes(region, sem):
        pltpu.make_async_copy(region, region, sem).wait()

    def sent_later(region, phase):
        unsent.append((region, send_sem.at[phase]))

    load_s = pltpu.make_async_copy(s_ref, s_v, local_sem.at[0])
    load_f = pltpu.make_async_copy(f_ref, f_v, local_sem.at[1])
    load_p = pltpu.make_async_copy(p_ref.at[own_share], pert, local_sem.at[2])
    own_f = [
        pltpu.make_async_copy(
            f_ref.at[rows_at(t * share + piece * part, part)],
            frow.at[pl.ds(piece * piece_rows, part)], local_sem.at[5 + piece],
        )
        for piece in range(PIECES)
    ]

    def half_rows(h, owner):
        return rows_at(h * half + owner * owned, owned)

    own_d = [
        pltpu.make_async_copy(d_ref.at[pl.ds(h * owned, owned)], dall.at[half_rows(h, o)], local_sem.at[(4, 9)[h]])
        for h in range(HALVES)
    ]

    barrier = pltpu.get_barrier_semaphore()
    for peer in tm_to[1:]:
        pl.semaphore_signal(barrier, inc=1, device_id={"tm": peer}, device_id_type=MESH)
    for peer in obs_to[1:]:
        pl.semaphore_signal(barrier, inc=1, device_id={"obs": peer}, device_id_type=MESH)

    load_f.start()
    for copy in own_f:
        copy.start()
    for copy in own_d:
        copy.start()
    load_p.start()
    load_s.start()
    pl.semaphore_wait(barrier, n_tm - 1 + n_obs - 1)

    z_peer = obs_at(0, 1)
    for h in range(HALVES):
        send(d_ref.at[pl.ds(h * owned, owned)], dall.at[half_rows(h, o)], DRAWS_Z, "obs", z_peer)
    sent_later(dall.at[pl.ds(0, draws)], DRAWS_Z)
    def send_footprints(piece):
        for r in range(1, n_tm):
            send(
                f_ref.at[rows_at(tm_to[r] * share + piece * part, part)],
                frow.at[pl.ds(piece * piece_rows + r * part, part)],
                FOOT, "tm", tm_to[r], frecv_sem.at[piece],
            )

    send_footprints(0)
    sent_later(frow.at[pl.ds(share, rows - share)], FOOT)
    for dy in range(1, 4):
        for h in range(HALVES):
            send(d_ref.at[pl.ds(h * owned, owned)], dall.at[half_rows(h, o)], DRAWS_Y, "obs", obs_at(dy, 0))
    await_bytes(dall.at[pl.ds(0, draws)], recv_sem.at[DRAWS_Z])
    for dy in range(1, 4):
        for h in range(HALVES):
            here = dall.at[half_rows(h, z_peer)]
            send(here, here, DRAWS_Y, "obs", obs_at(dy, 0))
    sent_later(dall.at[pl.ds(0, 6 * draws)], DRAWS_Y)

    load_f.wait()
    for copy in own_d:
        copy.wait()
    await_bytes(dall.at[pl.ds(0, 6 * draws)], recv_sem.at[DRAWS_Y])
    psend[...] = dot_nt(f_v[...], dall[...])
    for r in range(1, n_tm):
        send(psend.at[rows_at(tm_to[r] * share, share)], prow.at[pl.ds(r * share, share)], PRED, "tm", tm_to[r])
    sent_later(psend.at[pl.ds(share, rows - share)], PRED)
    for piece in range(1, PIECES):
        send_footprints(piece)

    def periods(shape, dim):
        slot = lax.broadcasted_iota(jnp.int32, shape, dim) // part
        period = jnp.zeros(shape, jnp.int32)
        for r in range(n_tm):
            period = jnp.where(slot == r, tm_from[r], period)
        return period

    pick = (periods((piece_rows, n_tm), 0) == lax.broadcasted_iota(jnp.int32, (piece_rows, n_tm), 1)).astype(F32)
    pick_t = (periods((n_tm, piece_rows), 1) == lax.broadcasted_iota(jnp.int32, (n_tm, piece_rows), 0)).astype(F32)
    picked = jnp.dot(t_ref[...], pick_t, precision=lax.Precision.HIGHEST, preferred_element_type=F32)
    full = jnp.dot(pick, picked, precision=lax.Precision.HIGHEST, preferred_element_type=F32)
    row_in = lax.rem(lax.broadcasted_iota(jnp.int32, (piece_rows, piece_rows), 0), part)
    col_in = lax.rem(lax.broadcasted_iota(jnp.int32, (piece_rows, piece_rows), 1), part)
    full = jnp.where(row_in == col_in, full, 0.0)
    high = full.astype(BF16)
    mixer[pl.ds(0, piece_rows), :] = high
    mixer[pl.ds(piece_rows, piece_rows), :] = (full - high.astype(F32)).astype(BF16)
    dacc[...] = jnp.zeros_like(dacc)

    def send_mixed(piece):
        pltpu.make_async_copy(
            mrow.at[pl.ds(piece * piece_rows, part)],
            mixed.at[rows_at(t * share + piece * part, part)], local_sem.at[7 + piece],
        ).start()
        for r in range(1, n_tm):
            send(
                mrow.at[pl.ds(piece * piece_rows + r * part, part)],
                mixed.at[rows_at(t * share + piece * part, part)], MIXED, "tm", tm_from[r],
            )

    load_s.wait()
    for piece in range(PIECES):
        own_f[piece].wait()
        await_bytes(frow.at[pl.ds(piece * piece_rows + part, piece_rows - part)], frecv_sem.at[piece])
        here = pl.ds(piece * piece_rows, piece_rows)

        @pl.loop(0, cells // TILE)
        def _(c):
            cols = pl.ds(pl.multiple_of(c * TILE, TILE), TILE)
            block = dot_nn(frow[here, :], s_v[:, cols]).astype(BF16)
            both = dot_nn(mixer[...], block)
            out = (both[:piece_rows] + both[piece_rows:]).astype(BF16)
            mrow[here, cols] = out
            product = out.astype(F32) * frow[here, cols].astype(F32)
            dacc[pl.ds(piece * part, part), :] += product.reshape(n_tm, part, TILE).sum(axis=0)

    load_p.wait()
    await_bytes(prow.at[pl.ds(share, rows - share)], recv_sem.at[PRED])
    predicted = psend[own_share, :]
    predicted += prow[pl.ds(share, rows - share), :].reshape(n_tm - 1, share, -1).sum(axis=0)
    at_row = lax.broadcasted_iota(jnp.int32, (share, rows), 0) + t * share
    at_col = lax.broadcasted_iota(jnp.int32, (share, rows), 1)
    error = jnp.where(at_row == at_col, jnp.broadcast_to(e_ref[...], (share, rows)), 0.0).sum(axis=1, keepdims=True)
    divisor = dacc[...].sum(axis=1, keepdims=True) + error
    column = lax.broadcasted_iota(jnp.int32, (n_obs * draws, n_obs * draws), 1)
    in_half = lax.rem(column, half)
    draw = in_half // owned * draws + column // half * owned + lax.rem(column, owned)
    order = (lax.broadcasted_iota(jnp.int32, column.shape, 0) == draw).astype(F32)
    ordered = jnp.dot(pert[...], order, precision=lax.Precision.HIGHEST, preferred_element_type=F32)
    whole = ordered - predicted
    residual = [whole[:, h * half:(h + 1) * half] for h in range(HALVES)]

    def send_weights(step, h, weights):
        wall[step, h, own_share, :] = weights.astype(BF16)
        here = wall.at[step, h, own_share]
        phase = WEIGHTS + step * HALVES + h
        for r in range(1, n_tm):
            send(here, here, phase, "tm", tm_to[r])
        sent_later(wall.at[step, h, pl.ds(share, rows - share)], phase)

    def receive_weights(step, h):
        await_bytes(wall.at[step, h, pl.ds(share, rows - share)], recv_sem.at[WEIGHTS + step * HALVES + h])
        wt[pl.ds(h * half, half), :] = wall[step, h].T

    def targets(step):
        if STAGED[step]:
            return [(dy, dz) for dz in (1, 0) for dy in (1, 3, 2)]
        return OBS_STEPS[1:]

    def back_project(step, h):
        receive_weights(step, h)

        source = f_v if step < SWEEPS else mixed
        gp[step, h] = dot_nn(wt[pl.ds(h * half, half), :], source[...]).astype(BF16)
        phase = PARTS + step * HALVES + h
        for slot, (dy, dz) in enumerate(targets(step)):
            send(
                gp.at[step, h, rows_at(obs_at(dy, dz) * owned, owned)],
                grs.at[step, h, pl.ds(slot * owned, owned)], phase, "obs",
                obs_at(dy, 0) if STAGED[step] else obs_at(dy, dz),
            )
        sent_later(grs.at[step, h, pl.ds(0, len(targets(step)) * owned)], phase)

    def line_sum(step, h, dz):
        total = gp[step, h, rows_at(obs_at(0, dz) * owned, owned), :].astype(F32)
        for slot, target in enumerate(targets(step)):
            if not STAGED[step] or target[1] == dz:
                total += grs[step, h, pl.ds(slot * owned, owned), :].astype(F32)
        return total

    def await_parts(step, h):
        await_bytes(grs.at[step, h, pl.ds(0, len(targets(step)) * owned)], recv_sem.at[PARTS + step * HALVES + h])

    def pass_parts(step, h):
        if not STAGED[step]:
            return
        await_parts(step, h)
        gz_send[step, h] = line_sum(step, h, 1).astype(BF16)
        phase = PARTS_Z + step * HALVES + h
        send(gz_send.at[step, h], gz.at[step, h], phase, "obs", z_peer)
        sent_later(gz_send.at[step, h], phase)

    def received_sum(step, h):
        if not STAGED[step]:
            await_parts(step, h)
            return line_sum(step, h, 0)
        await_bytes(gz.at[step, h], recv_sem.at[PARTS_Z + step * HALVES + h])
        return line_sum(step, h, 0) + gz[step, h].astype(F32)

    def sum_parts(step, h):
        here = gall.at[step, h, rows_at(o * owned, owned)]
        here[...] = received_sum(step, h).astype(BF16)
        phase = SUMS + step * HALVES + h
        if STAGED[step]:
            send(here, here, SUMS_Z + step * HALVES + h, "obs", z_peer)
            sent_later(here, SUMS_Z + step * HALVES + h)
            for dy in (1, 3, 2):
                send(here, here, phase, "obs", obs_at(dy, 0))
        else:
            for peer in obs_to[1:]:
                send(here, here, phase, "obs", peer)
        sent_later(grs.at[step, h, pl.ds(0, len(targets(step)) * owned)], phase)

    def pass_sums(step, h):
        if not STAGED[step]:
            return
        here = gall.at[step, h, rows_at(z_peer * owned, owned)]
        await_bytes(here, recv_sem.at[SUMS_Z + step * HALVES + h])
        for dy in (1, 3, 2):
            send(here, here, SUMS + step * HALVES + h, "obs", obs_at(dy, 0))

    def exchange(step):
        pass_parts(step, 0)
        pass_parts(step, 1)
        sum_parts(step, 0)
        pass_sums(step, 0)
        sum_parts(step, 1)
        pass_sums(step, 1)

    def project(step, h):
        await_bytes(grs.at[step, h, pl.ds(0, len(targets(step)) * owned)], recv_sem.at[SUMS + step * HALVES + h])
        ysend[step, h] = dot_nt(mixed[...], gall[step, h]).astype(BF16)
        phase = PRODUCTS + step * HALVES + h
        for r in range(1, n_tm):
            send(
                ysend.at[step, h, rows_at(tm_to[r] * share, share)],
                yrow.at[step, h, pl.ds(r * share, share)], phase, "tm", tm_to[r],
            )
        sent_later(ysend.at[step, h, pl.ds(share, rows - share)], phase)

    def correct(step, h):
        await_bytes(yrow.at[step, h, pl.ds(share, rows - share)], recv_sem.at[PRODUCTS + step * HALVES + h])
        product = ysend[step, h, own_share, :].astype(F32)
        received = yrow[step, h, pl.ds(share, rows - share), :].astype(F32)
        product += received.reshape(n_tm - 1, share, half).sum(axis=0)
        weights[h] = weights[h] + (residual[h] - product - error * weights[h]) / divisor
        send_weights(step + 1, h, weights[h])

    weights = [residual[h] / divisor for h in range(HALVES)]
    for h in range(HALVES):
        send_weights(0, h, weights[h])
    send_mixed(0)
    sent_later(mrow.at[pl.ds(share, rows - share)], MIXED)

    back_project(0, 0)
    back_project(0, 1)
    send_mixed(1)
    exchange(0)
    for piece in range(PIECES):
        pltpu.make_async_copy(
            mrow.at[pl.ds(0, part)], mixed.at[pl.ds(0, part)], local_sem.at[7 + piece]
        ).wait()
    await_bytes(mixed.at[pl.ds(share, rows - share)], recv_sem.at[MIXED])
    for step in range(SWEEPS):
        project(step, 0)
        project(step, 1)
        correct(step, 0)
        correct(step, 1)
        back_project(step + 1, 0)
        back_project(step + 1, 1)
        if step < SWEEPS - 1:
            exchange(step + 1)

    for h in range(HALVES):
        pass_parts(SWEEPS, h)
    last = jnp.concatenate(weights, axis=1)
    w_ref[...] = lax.dot_general(
        last, order, (((1,), (1,)), ((), ())), precision=lax.Precision.HIGHEST, preferred_element_type=F32
    )
    for h in range(HALVES):
        u_ref[pl.ds(h * owned, owned), 0, :] = received_sum(SWEEPS, h)

    for region, sem in unsent:
        await_bytes(region, sem)


def body(n_obs, n_tm, footprints, spatial_cov, time_cov, flux_draws, perturbed, obs_error):
    rows, _, cells = footprints.shape
    own_draws = flux_draws.shape[0]
    draws = own_draws * n_obs
    share = rows // n_tm
    half = draws // HALVES
    any_space = pl.BlockSpec(memory_space=pl.ANY)
    vmem = pl.BlockSpec(memory_space=pltpu.VMEM)
    weights, update = pl.pallas_call(
        functools.partial(kernel, n_obs, n_tm),
        out_shape=(
            jax.ShapeDtypeStruct((share, draws), F32),
            jax.ShapeDtypeStruct((own_draws, 1, cells), F32),
        ),
        in_specs=[any_space, any_space, vmem, any_space, any_space, vmem],
        out_specs=(vmem, vmem),
        scratch_shapes=[
            pltpu.VMEM((rows, cells), BF16),
            pltpu.VMEM((cells, cells), BF16),
            pltpu.VMEM((rows, cells), BF16),
            pltpu.VMEM((rows, cells), BF16),
            pltpu.VMEM((rows, cells), BF16),
            pltpu.VMEM((draws, cells), BF16),
            pltpu.VMEM((rows, draws), F32),
            pltpu.VMEM((rows, draws), F32),
            pltpu.VMEM((SWEEPS + 1, HALVES, rows, half), BF16),
            pltpu.VMEM((draws, rows), BF16),
            pltpu.VMEM((SWEEPS + 1, HALVES, half, cells), BF16),
            pltpu.VMEM((SWEEPS + 1, HALVES, 7 * half // n_obs, cells), BF16),
            pltpu.VMEM((SWEEPS + 1, HALVES, half // n_obs, cells), BF16),
            pltpu.VMEM((SWEEPS + 1, HALVES, half // n_obs, cells), BF16),
            pltpu.VMEM((SWEEPS, HALVES, half, cells), BF16),
            pltpu.VMEM((SWEEPS, HALVES, rows, half), BF16),
            pltpu.VMEM((SWEEPS, HALVES, rows, half), BF16),
            pltpu.VMEM((2 * rows // PIECES, rows // PIECES), BF16),
            pltpu.VMEM((share, draws), F32),
            pltpu.VMEM((share, TILE), F32),
            pltpu.SemaphoreType.DMA((10,)),
            pltpu.SemaphoreType.DMA((EXCHANGES,)),
            pltpu.SemaphoreType.DMA((EXCHANGES,)),
            pltpu.SemaphoreType.DMA((PIECES,)),
        ],
        compiler_params=pltpu.CompilerParams(
            collective_id=0, has_side_effects=True, vmem_limit_bytes=56 * 1024 * 1024
        ),
    )(
        footprints[:, 0, :], spatial_cov, time_cov, flux_draws[:, 0, :],
        perturbed, obs_error[None, :],
    )
    return weights, update


def solution(mesh):
    n_obs, n_tm = mesh.shape["obs"], mesh.shape["tm"]
    in_specs = (P("obs", "tm", None), P(), P(), P("obs", "tm", None), P("obs", None), P("obs"))
    out_specs = (P(("obs", "tm"), None), P("obs", "tm", None))
    return jax.shard_map(
        functools.partial(body, n_obs, n_tm), mesh=mesh, in_specs=in_specs, out_specs=out_specs, check_vma=False
    )
```

```python
import functools

import jax
import jax.numpy as jnp
from jax import lax
from jax.experimental import pallas as pl
from jax.experimental.pallas import tpu as pltpu
from jax.sharding import PartitionSpec as P

SWEEPS = 2
MESH = pl.DeviceIdType.MESH
BF16 = jnp.bfloat16
F32 = jnp.float32
TILE = 1024
PIECES = 2
HALVES = 2
STAGED = (True, False, False)
DRAWS_Z, DRAWS_Y, FOOT, PRED, MIXED = range(5)
WEIGHTS = 5
PARTS = WEIGHTS + (SWEEPS + 1) * HALVES
PARTS_Z = PARTS + (SWEEPS + 1) * HALVES
SUMS_Z = PARTS_Z + (SWEEPS + 1) * HALVES
SUMS = SUMS_Z + SWEEPS * HALVES
PRODUCTS = SUMS + SWEEPS * HALVES
EXCHANGES = PRODUCTS + SWEEPS * HALVES
TM_STEPS = (
    (0, 0, 0), (1, 0, 0), (3, 0, 0), (0, 1, 0), (2, 0, 0), (1, 1, 0), (3, 1, 0), (0, 1, 1),
    (2, 1, 0), (1, 0, 1), (3, 0, 1), (2, 0, 1), (1, 1, 1), (3, 1, 1), (2, 1, 1), (0, 0, 1),
)
OBS_STEPS = ((0, 0), (1, 0), (3, 0), (0, 1), (2, 0), (1, 1), (3, 1), (2, 1))


def dot_nt(left, right):
    return lax.dot_general(left, right, (((1,), (1,)), ((), ())), preferred_element_type=F32)


def dot_nn(left, right):
    return jnp.dot(left, right, preferred_element_type=F32)


def rows_at(start, size):
    return pl.ds(pl.multiple_of(start, size), size)


def kernel(
    n_obs, n_tm,
    f_ref, s_ref, t_ref, d_ref, p_ref, e_ref,
    w_ref, u_ref,
    f_v, s_v, frow, mrow, mixed, dall, psend, prow,
    wall, wt, gp, grs, gz_send, gz, gall, ysend, yrow, mixer, pert, dacc,
    local_sem, send_sem, recv_sem, frecv_sem,
):
    o = lax.axis_index("obs")
    t = lax.axis_index("tm")
    rows, cells = f_ref.shape
    share = rows // n_tm
    draws = d_ref.shape[0]
    part = share // PIECES
    piece_rows = rows // PIECES
    half = draws * n_obs // HALVES
    owned = half // n_obs
    x, z_far, core = t // 4, lax.rem(t // 2, 2), lax.rem(t, 2)
    z_near, y = o // 4, lax.rem(o, 4)

    def tm_at(dx, dz, dc):
        return lax.rem(x + dx, 4) * 4 + lax.rem(z_far + dz, 2) * 2 + lax.rem(core + dc, 2)

    def obs_at(dy, dz):
        return lax.rem(z_near + dz, 2) * 4 + lax.rem(y + dy, 4)

    tm_to = [tm_at(*step) for step in TM_STEPS]
    tm_from = [tm_at(4 - dx, dz, dc) for dx, dz, dc in TM_STEPS]
    obs_to = [obs_at(*step) for step in OBS_STEPS]
    own_share = rows_at(t * share, share)

    unsent = []

    def send(src, dst, phase, axis, peer, recv=None):
        pltpu.make_async_remote_copy(
            src_ref=src, dst_ref=dst, send_sem=send_sem.at[phase],
            recv_sem=recv_sem.at[phase] if recv is None else recv,
            device_id={axis: peer}, device_id_type=MESH,
        ).start()

    def await_bytes(region, sem):
        pltpu.make_async_copy(region, region, sem).wait()

    def sent_later(region, phase):
        unsent.append((region, send_sem.at[phase]))

    load_s = pltpu.make_async_copy(s_ref, s_v, local_sem.at[0])
    load_f = pltpu.make_async_copy(f_ref, f_v, local_sem.at[1])
    load_p = pltpu.make_async_copy(p_ref.at[own_share], pert, local_sem.at[2])
    own_f = [
        pltpu.make_async_copy(
            f_ref.at[rows_at(t * share + piece * part, part)],
            frow.at[pl.ds(piece * piece_rows, part)], local_sem.at[5 + piece],
        )
        for piece in range(PIECES)
    ]

    def half_rows(h, owner):
        return rows_at(h * half + owner * owned, owned)

    own_d = [
        pltpu.make_async_copy(d_ref.at[pl.ds(h * owned, owned)], dall.at[half_rows(h, o)], local_sem.at[(4, 9)[h]])
        for h in range(HALVES)
    ]

    barrier = pltpu.get_barrier_semaphore()
    for peer in tm_to[1:]:
        pl.semaphore_signal(barrier, inc=1, device_id={"tm": peer}, device_id_type=MESH)
    for peer in obs_to[1:]:
        pl.semaphore_signal(barrier, inc=1, device_id={"obs": peer}, device_id_type=MESH)

    load_f.start()
    for copy in own_f:
        copy.start()
    for copy in own_d:
        copy.start()
    load_p.start()
    load_s.start()
    pl.semaphore_wait(barrier, n_tm - 1 + n_obs - 1)

    z_peer = obs_at(0, 1)
    for h in range(HALVES):
        send(d_ref.at[pl.ds(h * owned, owned)], dall.at[half_rows(h, o)], DRAWS_Z, "obs", z_peer)
    sent_later(dall.at[pl.ds(0, draws)], DRAWS_Z)
    def send_footprints(piece):
        for r in range(1, n_tm):
            send(
                f_ref.at[rows_at(tm_to[r] * share + piece * part, part)],
                frow.at[pl.ds(piece * piece_rows + r * part, part)],
                FOOT, "tm", tm_to[r], frecv_sem.at[piece],
            )

    send_footprints(0)
    sent_later(frow.at[pl.ds(share, rows - share)], FOOT)
    for dy in range(1, 4):
        for h in range(HALVES):
            send(d_ref.at[pl.ds(h * owned, owned)], dall.at[half_rows(h, o)], DRAWS_Y, "obs", obs_at(dy, 0))
    await_bytes(dall.at[pl.ds(0, draws)], recv_sem.at[DRAWS_Z])
    for dy in range(1, 4):
        for h in range(HALVES):
            here = dall.at[half_rows(h, z_peer)]
            send(here, here, DRAWS_Y, "obs", obs_at(dy, 0))
    sent_later(dall.at[pl.ds(0, 6 * draws)], DRAWS_Y)

    load_f.wait()
    for copy in own_d:
        copy.wait()
    await_bytes(dall.at[pl.ds(0, 6 * draws)], recv_sem.at[DRAWS_Y])
    psend[...] = dot_nt(f_v[...], dall[...])
    for r in range(1, n_tm):
        send(psend.at[rows_at(tm_to[r] * share, share)], prow.at[pl.ds(r * share, share)], PRED, "tm", tm_to[r])
    sent_later(psend.at[pl.ds(share, rows - share)], PRED)
    for piece in range(1, PIECES):
        send_footprints(piece)

    def periods(shape, dim):
        slot = lax.broadcasted_iota(jnp.int32, shape, dim) // part
        period = jnp.zeros(shape, jnp.int32)
        for r in range(n_tm):
            period = jnp.where(slot == r, tm_from[r], period)
        return period

    pick = (periods((piece_rows, n_tm), 0) == lax.broadcasted_iota(jnp.int32, (piece_rows, n_tm), 1)).astype(F32)
    pick_t = (periods((n_tm, piece_rows), 1) == lax.broadcasted_iota(jnp.int32, (n_tm, piece_rows), 0)).astype(F32)
    picked = jnp.dot(t_ref[...], pick_t, precision=lax.Precision.HIGHEST, preferred_element_type=F32)
    full = jnp.dot(pick, picked, precision=lax.Precision.HIGHEST, preferred_element_type=F32)
    row_in = lax.rem(lax.broadcasted_iota(jnp.int32, (piece_rows, piece_rows), 0), part)
    col_in = lax.rem(lax.broadcasted_iota(jnp.int32, (piece_rows, piece_rows), 1), part)
    full = jnp.where(row_in == col_in, full, 0.0)
    high = full.astype(BF16)
    mixer[pl.ds(0, piece_rows), :] = high
    mixer[pl.ds(piece_rows, piece_rows), :] = (full - high.astype(F32)).astype(BF16)
    dacc[...] = jnp.zeros_like(dacc)

    def send_mixed(piece):
        pltpu.make_async_copy(
            mrow.at[pl.ds(piece * piece_rows, part)],
            mixed.at[rows_at(t * share + piece * part, part)], local_sem.at[7 + piece],
        ).start()
        for r in range(1, n_tm):
            send(
                mrow.at[pl.ds(piece * piece_rows + r * part, part)],
                mixed.at[rows_at(t * share + piece * part, part)], MIXED, "tm", tm_from[r],
            )

    load_p.wait()
    at_row = lax.broadcasted_iota(jnp.int32, (share, rows), 0) + t * share
    at_col = lax.broadcasted_iota(jnp.int32, (share, rows), 1)
    error = jnp.where(at_row == at_col, jnp.broadcast_to(e_ref[...], (share, rows)), 0.0).sum(axis=1, keepdims=True)
    column = lax.broadcasted_iota(jnp.int32, (n_obs * draws, n_obs * draws), 1)
    in_half = lax.rem(column, half)
    draw = in_half // owned * draws + column // half * owned + lax.rem(column, owned)
    order = (lax.broadcasted_iota(jnp.int32, column.shape, 0) == draw).astype(F32)
    ordered = jnp.dot(pert[...], order, precision=lax.Precision.HIGHEST, preferred_element_type=F32)
    load_s.wait()
    for piece in range(PIECES):
        own_f[piece].wait()
        await_bytes(frow.at[pl.ds(piece * piece_rows + part, piece_rows - part)], frecv_sem.at[piece])
        here = pl.ds(piece * piece_rows, piece_rows)

        @pl.loop(0, cells // TILE)
        def _(c):
            cols = pl.ds(pl.multiple_of(c * TILE, TILE), TILE)
            block = dot_nn(frow[here, :], s_v[:, cols]).astype(BF16)
            both = dot_nn(mixer[...], block)
            out = (both[:piece_rows] + both[piece_rows:]).astype(BF16)
            mrow[here, cols] = out
            product = out.astype(F32) * frow[here, cols].astype(F32)
            dacc[pl.ds(piece * part, part), :] += product.reshape(n_tm, part, TILE).sum(axis=0)

    await_bytes(prow.at[pl.ds(share, rows - share)], recv_sem.at[PRED])
    predicted = psend[own_share, :]
    predicted += prow[pl.ds(share, rows - share), :].reshape(n_tm - 1, share, -1).sum(axis=0)
    divisor = dacc[...].sum(axis=1, keepdims=True) + error
    whole = ordered - predicted
    residual = [whole[:, h * half:(h + 1) * half] for h in range(HALVES)]

    def send_weights(step, h, weights):
        wall[step, h, own_share, :] = weights.astype(BF16)
        here = wall.at[step, h, own_share]
        phase = WEIGHTS + step * HALVES + h
        for r in range(1, n_tm):
            send(here, here, phase, "tm", tm_to[r])
        sent_later(wall.at[step, h, pl.ds(share, rows - share)], phase)

    def receive_weights(step, h):
        await_bytes(wall.at[step, h, pl.ds(share, rows - share)], recv_sem.at[WEIGHTS + step * HALVES + h])
        wt[pl.ds(h * half, half), :] = wall[step, h].T

    def targets(step):
        if STAGED[step]:
            return [(dy, dz) for dz in (1, 0) for dy in (1, 3, 2)]
        return OBS_STEPS[1:]

    def back_project(step, h):
        receive_weights(step, h)

        source = f_v if step < SWEEPS else mixed
        gp[step, h] = dot_nn(wt[pl.ds(h * half, half), :], source[...]).astype(BF16)
        phase = PARTS + step * HALVES + h
        for slot, (dy, dz) in enumerate(targets(step)):
            send(
                gp.at[step, h, rows_at(obs_at(dy, dz) * owned, owned)],
                grs.at[step, h, pl.ds(slot * owned, owned)], phase, "obs",
                obs_at(dy, 0) if STAGED[step] else obs_at(dy, dz),
            )
        sent_later(grs.at[step, h, pl.ds(0, len(targets(step)) * owned)], phase)

    def line_sum(step, h, dz):
        total = gp[step, h, rows_at(obs_at(0, dz) * owned, owned), :].astype(F32)
        for slot, target in enumerate(targets(step)):
            if not STAGED[step] or target[1] == dz:
                total += grs[step, h, pl.ds(slot * owned, owned), :].astype(F32)
        return total

    def await_parts(step, h):
        await_bytes(grs.at[step, h, pl.ds(0, len(targets(step)) * owned)], recv_sem.at[PARTS + step * HALVES + h])

    def pass_parts(step, h):
        if not STAGED[step]:
            return
        await_parts(step, h)
        gz_send[step, h] = line_sum(step, h, 1).astype(BF16)
        phase = PARTS_Z + step * HALVES + h
        send(gz_send.at[step, h], gz.at[step, h], phase, "obs", z_peer)
        sent_later(gz_send.at[step, h], phase)

    def received_sum(step, h):
        if not STAGED[step]:
            await_parts(step, h)
            return line_sum(step, h, 0)
        await_bytes(gz.at[step, h], recv_sem.at[PARTS_Z + step * HALVES + h])
        return line_sum(step, h, 0) + gz[step, h].astype(F32)

    def sum_parts(step, h):
        here = gall.at[step, h, rows_at(o * owned, owned)]
        here[...] = received_sum(step, h).astype(BF16)
        phase = SUMS + step * HALVES + h
        if STAGED[step]:
            send(here, here, SUMS_Z + step * HALVES + h, "obs", z_peer)
            sent_later(here, SUMS_Z + step * HALVES + h)
            for dy in (1, 3, 2):
                send(here, here, phase, "obs", obs_at(dy, 0))
        else:
            for peer in obs_to[1:]:
                send(here, here, phase, "obs", peer)
        sent_later(grs.at[step, h, pl.ds(0, len(targets(step)) * owned)], phase)

    def pass_sums(step, h):
        if not STAGED[step]:
            return
        here = gall.at[step, h, rows_at(z_peer * owned, owned)]
        await_bytes(here, recv_sem.at[SUMS_Z + step * HALVES + h])
        for dy in (1, 3, 2):
            send(here, here, SUMS + step * HALVES + h, "obs", obs_at(dy, 0))

    def exchange(step):
        pass_parts(step, 0)
        pass_parts(step, 1)
        sum_parts(step, 0)
        pass_sums(step, 0)
        sum_parts(step, 1)
        pass_sums(step, 1)

    def project(step, h):
        await_bytes(grs.at[step, h, pl.ds(0, len(targets(step)) * owned)], recv_sem.at[SUMS + step * HALVES + h])
        ysend[step, h] = dot_nt(mixed[...], gall[step, h]).astype(BF16)
        phase = PRODUCTS + step * HALVES + h
        for r in range(1, n_tm):
            send(
                ysend.at[step, h, rows_at(tm_to[r] * share, share)],
                yrow.at[step, h, pl.ds(r * share, share)], phase, "tm", tm_to[r],
            )
        sent_later(ysend.at[step, h, pl.ds(share, rows - share)], phase)

    def correct(step, h):
        await_bytes(yrow.at[step, h, pl.ds(share, rows - share)], recv_sem.at[PRODUCTS + step * HALVES + h])
        product = ysend[step, h, own_share, :].astype(F32)
        received = yrow[step, h, pl.ds(share, rows - share), :].astype(F32)
        product += received.reshape(n_tm - 1, share, half).sum(axis=0)
        weights[h] = weights[h] + (residual[h] - product - error * weights[h]) / divisor
        send_weights(step + 1, h, weights[h])

    weights = [residual[h] / divisor for h in range(HALVES)]
    for h in range(HALVES):
        send_weights(0, h, weights[h])
    send_mixed(0)
    sent_later(mrow.at[pl.ds(share, rows - share)], MIXED)

    back_project(0, 0)
    back_project(0, 1)
    send_mixed(1)
    exchange(0)
    for piece in range(PIECES):
        pltpu.make_async_copy(
            mrow.at[pl.ds(0, part)], mixed.at[pl.ds(0, part)], local_sem.at[7 + piece]
        ).wait()
    await_bytes(mixed.at[pl.ds(share, rows - share)], recv_sem.at[MIXED])
    for step in range(SWEEPS):
        project(step, 0)
        project(step, 1)
        correct(step, 0)
        correct(step, 1)
        back_project(step + 1, 0)
        back_project(step + 1, 1)
        if step < SWEEPS - 1:
            exchange(step + 1)

    for h in range(HALVES):
        pass_parts(SWEEPS, h)
    last = jnp.concatenate(weights, axis=1)
    w_ref[...] = lax.dot_general(
        last, order, (((1,), (1,)), ((), ())), precision=lax.Precision.HIGHEST, preferred_element_type=F32
    )
    for h in range(HALVES):
        u_ref[pl.ds(h * owned, owned), 0, :] = received_sum(SWEEPS, h)

    for region, sem in unsent:
        await_bytes(region, sem)


def body(n_obs, n_tm, footprints, spatial_cov, time_cov, flux_draws, perturbed, obs_error):
    rows, _, cells = footprints.shape
    own_draws = flux_draws.shape[0]
    draws = own_draws * n_obs
    share = rows // n_tm
    half = draws // HALVES
    any_space = pl.BlockSpec(memory_space=pl.ANY)
    vmem = pl.BlockSpec(memory_space=pltpu.VMEM)
    weights, update = pl.pallas_call(
        functools.partial(kernel, n_obs, n_tm),
        out_shape=(
            jax.ShapeDtypeStruct((share, draws), F32),
            jax.ShapeDtypeStruct((own_draws, 1, cells), F32),
        ),
        in_specs=[any_space, any_space, vmem, any_space, any_space, vmem],
        out_specs=(vmem, vmem),
        scratch_shapes=[
            pltpu.VMEM((rows, cells), BF16),
            pltpu.VMEM((cells, cells), BF16),
            pltpu.VMEM((rows, cells), BF16),
            pltpu.VMEM((rows, cells), BF16),
            pltpu.VMEM((rows, cells), BF16),
            pltpu.VMEM((draws, cells), BF16),
            pltpu.VMEM((rows, draws), F32),
            pltpu.VMEM((rows, draws), F32),
            pltpu.VMEM((SWEEPS + 1, HALVES, rows, half), BF16),
            pltpu.VMEM((draws, rows), BF16),
            pltpu.VMEM((SWEEPS + 1, HALVES, half, cells), BF16),
            pltpu.VMEM((SWEEPS + 1, HALVES, 7 * half // n_obs, cells), BF16),
            pltpu.VMEM((SWEEPS + 1, HALVES, half // n_obs, cells), BF16),
            pltpu.VMEM((SWEEPS + 1, HALVES, half // n_obs, cells), BF16),
            pltpu.VMEM((SWEEPS, HALVES, half, cells), BF16),
            pltpu.VMEM((SWEEPS, HALVES, rows, half), BF16),
            pltpu.VMEM((SWEEPS, HALVES, rows, half), BF16),
            pltpu.VMEM((2 * rows // PIECES, rows // PIECES), BF16),
            pltpu.VMEM((share, draws), F32),
            pltpu.VMEM((share, TILE), F32),
            pltpu.SemaphoreType.DMA((10,)),
            pltpu.SemaphoreType.DMA((EXCHANGES,)),
            pltpu.SemaphoreType.DMA((EXCHANGES,)),
            pltpu.SemaphoreType.DMA((PIECES,)),
        ],
        compiler_params=pltpu.CompilerParams(
            collective_id=0, has_side_effects=True, vmem_limit_bytes=56 * 1024 * 1024
        ),
    )(
        footprints[:, 0, :], spatial_cov, time_cov, flux_draws[:, 0, :],
        perturbed, obs_error[None, :],
    )
    return weights, update


def solution(mesh):
    n_obs, n_tm = mesh.shape["obs"], mesh.shape["tm"]
    in_specs = (P("obs", "tm", None), P(), P(), P("obs", "tm", None), P("obs", None), P("obs"))
    out_specs = (P(("obs", "tm"), None), P("obs", "tm", None))
    return jax.shard_map(
        functools.partial(body, n_obs, n_tm), mesh=mesh, in_specs=in_specs, out_specs=out_specs, check_vma=False
    )
```
